256 devices in a mesh: samp: 16 (over z_hi, x, core), gene: 4 (over z_lo), snp: 4 (over y).
Axes of the slice: x: 4, y: 4, z: 8 (z_hi: 2, z_lo: 4; z = z_hi * 4 + z_lo), core: 2. Of those that a mesh axis runs over, the one named last changes fastest.
Arguments:
- expression: bfloat16 [4096, 16384], P('samp', ('gene', 'snp')), may hold values from -6 to 6
- loadings: bfloat16 [16384, 128], P(('gene', 'snp')), may hold values from -0.046875 to 0.046875
- dosage: bfloat16 [4096, 16384], P(None, ('gene', 'snp')), may hold values from 0 to 2
Outputs:
- assoc: bfloat16 [16, 16, 64, 16384], P(None, 'samp', None, ('gene', 'snp'))
The draws below stay inside these ranges and needn't reach their ends.
All inputs are finite; a program needn't handle non-finite values.
Results may differ from the reference program's by a relative error of at most 0.0065.
Values may be sent and summed in bfloat16 or wider, within the bound.
No kernel may reach another device: no remote copies, remote signals or barrier semaphores. Data moves between devices by JAX's collectives and lax.ppermute only.
A program may use at most 64 MiB of HBM per device.

```python
import jax
import jax.numpy as jnp
from jax import lax

K = 128
GP = 64
S = 4096
BLOCKS = 16
G_LOC = 1024
G = 16384
P_SIZE = 16384
N_SAMP = 16


def shard_levels(own_key, shape, pieces, low, high):
    gain, own = 1.0, jax.random.fold_in(own_key, 6)
    for axis_at, shards_of in pieces:
        steps = jnp.exp(jax.random.uniform(jax.random.fold_in(own, axis_at), (shards_of,), jnp.float32, low / len(pieces), high / len(pieces)))
        gain = gain * jnp.repeat(steps, shape[axis_at] // shards_of).reshape([-1 if axis == axis_at else 1 for axis in range(len(shape))])
    return gain


def bell_draw(rng, dims, deviation, most, pieces=(), kind=jnp.bfloat16):
    factor_of = shard_levels(rng, dims, pieces, -0.22, 0.18) if pieces else 1.0
    drawn = jax.random.normal(rng, dims, jnp.float32) * deviation * factor_of
    return jnp.minimum(jnp.maximum(drawn, -most), most).astype(kind)


def setup_inputs(seed: int = 0) -> dict:
    arg_keys = jax.random.split(jax.random.key(seed), 4)
    return {
        "expression": bell_draw(arg_keys[0], (S, G), 1.0, 6.0, ((0, 16), (1, 16))),
        "loadings": bell_draw(arg_keys[1], (G, K), G ** -0.5, 0.046875, ((0, 16),)),
        "dosage": jnp.clip(2.0 * jax.random.uniform(arg_keys[2], (S, P_SIZE), jnp.float32) ** shard_levels(arg_keys[2], (S, P_SIZE), ((1, 16),), -0.2, 0.2), 0.0, 2.0).astype(jnp.bfloat16),
    }


ridge_factor = 1.0
ridge_sample = 1.0

def reference(expression, loadings, dosage):
    contract = (((0,), (0,)), ((), ()))
    identity = jnp.eye(K, dtype=jnp.float32)
    factor_sum = jnp.dot(expression.astype(jnp.float32), loadings.astype(jnp.float32), preferred_element_type=jnp.float32)
    gram = lax.dot_general(loadings.astype(jnp.float32), loadings.astype(jnp.float32), contract, preferred_element_type=jnp.float32) + ridge_factor * identity
    lower_gram = jnp.linalg.cholesky(gram)
    factors = jax.scipy.linalg.cho_solve((lower_gram, True), factor_sum.T).T.astype(jnp.bfloat16)
    hessian = lax.dot_general(factors.astype(jnp.float32), factors.astype(jnp.float32), contract, preferred_element_type=jnp.float32) + ridge_sample * identity
    cross = lax.dot_general(factors.astype(jnp.float32), expression.astype(jnp.float32), contract, preferred_element_type=jnp.float32)
    lower_hess = jnp.linalg.cholesky(hessian)
    fit_coef = jax.scipy.linalg.cho_solve((lower_hess, True), cross).astype(jnp.bfloat16)
    fitted = lax.dot_general(fit_coef.astype(jnp.float32), factors.astype(jnp.float32), (((0,), (1,)), ((), ())), preferred_element_type=jnp.float32)
    residual_t = (expression.T.astype(jnp.float32) - fitted).astype(jnp.bfloat16)
    norm_scale = 1.0 / jnp.sqrt(jnp.float32(S))
    gene_blocks = residual_t.reshape(BLOCKS, G_LOC, S)

    def block_scores(block_rows):
        return (jnp.dot(block_rows.astype(jnp.float32), dosage.astype(jnp.float32), preferred_element_type=jnp.float32) * norm_scale).astype(jnp.bfloat16)
    scores = lax.map(block_scores, gene_blocks)
    return scores.reshape(BLOCKS, N_SAMP, GP, P_SIZE)
```

```python
import jax
import jax.numpy as jnp
import numpy as np
from jax import lax
from jax.sharding import Mesh, PartitionSpec as P

ridge_factor = 1.0
ridge_sample = 1.0
SAMP = ("zh", "x", "core")
COLS = ("zl", "y")
HI = lax.Precision.HIGHEST


def shift(array, axis, by, wrap):
    size = lax.axis_size(axis)
    pairs = [(i, (i + by) % size) for i in range(size) if wrap or 0 <= i + by < size]
    return lax.ppermute(array, axis, pairs)


def z_gather(piece):
    at = lax.axis_index("zl")
    right, left = [piece], [piece]
    for _ in range(3):
        right.append(shift(right[-1], "zl", 1, False))
        left.append(shift(left[-1], "zl", -1, False))
    slots = [piece] + [jnp.where(at >= k, right[k], left[4 - k]) for k in (1, 2, 3)]
    return jnp.stack(slots)


def y_gather(stack):
    ahead = shift(stack, "y", 1, True)
    behind = shift(stack, "y", -1, True)
    half = stack.shape[0] // 2
    far_low = shift(ahead[:half], "y", 1, True)
    far_high = shift(behind[half:], "y", -1, True)
    return [stack, ahead, jnp.concatenate([far_low, far_high]), behind]


def body(expression, loadings, dosage):
    contract = (((0,), (0,)), ((), ()))
    samples, genes = expression.shape
    factor_count = loadings.shape[1]
    n_samp = lax.axis_size(SAMP)
    n_cols = lax.axis_size(COLS)
    panel = genes // n_samp
    all_samples, snps = dosage.shape
    identity = jnp.eye(factor_count, dtype=jnp.float32)
    norm_scale = 1.0 / jnp.sqrt(jnp.float32(all_samples))

    mine = lax.all_to_all(expression.T.reshape(n_samp, panel, samples), SAMP, 0, 0, tiled=True)
    parts = [y_gather(z_gather(mine[:, i * 32 : i * 32 + 32])) for i in range(2)]

    local_factor = jnp.dot(expression, loadings, preferred_element_type=jnp.float32)
    local_gram = lax.dot_general(loadings, loadings, contract, preferred_element_type=jnp.float32)
    both = jnp.concatenate(
        [
            local_factor.reshape(n_cols, samples // n_cols, factor_count),
            local_gram.reshape(n_cols, factor_count // n_cols, factor_count),
        ],
        axis=1,
    )
    both = lax.all_to_all(both, COLS, 0, 0, tiled=True).sum(axis=0)
    both = lax.all_to_all(jnp.broadcast_to(both[None], (n_cols,) + both.shape), COLS, 0, 0, tiled=True)
    cut = samples // n_cols
    factor_sum = both[:, :cut].reshape(samples, factor_count)
    gram_sum = both[:, cut:].reshape(factor_count, factor_count)
    lower_gram = jnp.linalg.cholesky(gram_sum + ridge_factor * identity)
    factors = jax.scipy.linalg.cho_solve((lower_gram, True), factor_sum.T).T.astype(jnp.bfloat16)
    factors = lax.all_to_all(jnp.broadcast_to(factors[None], (n_samp,) + factors.shape), SAMP, 0, 0, tiled=True)
    flat = factors.reshape(all_samples, factor_count)

    hess = lax.dot_general(flat, flat, contract, preferred_element_type=jnp.float32)
    lower_hess = jnp.linalg.cholesky(hess + ridge_sample * identity)
    f_dosage = lax.dot_general(flat, dosage, contract, preferred_element_type=jnp.float32)

    dos3 = dosage.reshape(n_samp, samples, snps)
    outs = []
    for part in parts:
        for stack in part:
            rows = stack.transpose(0, 2, 1, 3).reshape(-1, all_samples)
            score = jnp.dot(rows, dosage, preferred_element_type=jnp.float32)
            cross = jnp.dot(rows, flat, preferred_element_type=jnp.float32)
            coef = jax.scipy.linalg.cho_solve((lower_hess, True), cross.T).T.astype(jnp.bfloat16)
            fit = jnp.dot(coef.astype(jnp.float32), f_dosage, preferred_element_type=jnp.float32, precision=HI)
            outs.append(((score - fit) * norm_scale).astype(jnp.bfloat16).reshape(4, 1, 32, snps))
    at_z, at_y = lax.axis_index("zl"), lax.axis_index("y")
    out = jnp.zeros((4, 4, 1, panel, snps), jnp.bfloat16)
    for c in range(2):
        for m in range(4):
            for k in range(4):
                out = lax.dynamic_update_slice(
                    out, outs[c * 4 + m][k][None, None],
                    ((at_z - k) % 4, (at_y - m) % 4, 0, 32 * c, 0))
    return out.reshape(n_cols, 1, panel, snps)


def solution(mesh):
    fine = Mesh(mesh.devices.reshape(2, 4, 2, 4, 4), SAMP + COLS)
    placed = (P(SAMP, COLS), P(COLS, None), P(None, COLS))
    return jax.shard_map(
        body, mesh=fine, in_specs=placed, out_specs=P(None, SAMP, None, COLS), check_vma=False
    )
```

```python
import functools

import jax
import jax.numpy as jnp
from jax import lax
from jax.experimental import pallas as pl
from jax.experimental.pallas import tpu as pltpu
from jax.sharding import Mesh, PartitionSpec as P

ridge_factor = 1.0
ridge_sample = 1.0
SAMP = ("zh", "x", "core")
COLS = ("zl", "y")
CHUNKS = 4
F32 = jnp.float32
BF16 = jnp.bfloat16
HI = lax.Precision.HIGHEST
NT = (((1,), (1,)), ((), ()))
TN = (((0,), (0,)), ((), ()))


def cycle(array, axis, by):
    size = lax.axis_size(axis)
    return lax.ppermute(array, axis, [(i, (i + by) % size) for i in range(size)])


def invert2(a, b, c):
    r = 1.0 / (a * c - b * b)
    return c * r, -b * r, a * r


def sweep(a_ref):
    n = a_ref.shape[0]
    ci = lax.broadcasted_iota(jnp.int32, (n, n), 1)
    lane = ci[:1]

    def step(t, _):
        k = 4 * t
        a = a_ref[...]
        r = [a_ref[pl.ds(k + i, 1), :] for i in range(4)]
        c = [jnp.sum(jnp.where(ci == k + i, a, 0.0), axis=1, keepdims=True) for i in range(4)]
        b = [[None] * i + [jnp.sum(jnp.where(lane == k + j, r[i], 0.0), axis=1, keepdims=True) for j in range(i, 4)] for i in range(4)]
        s11, s12, s22 = invert2(b[0][0], b[0][1], b[1][1])
        q11, q12, q21, q22 = b[0][2], b[0][3], b[1][2], b[1][3]
        w11, w12 = s11 * q11 + s12 * q21, s11 * q12 + s12 * q22
        w21, w22 = s12 * q11 + s22 * q21, s12 * q12 + s22 * q22
        t11, t12, t22 = invert2(
            b[2][2] - (q11 * w11 + q21 * w21), b[2][3] - (q11 * w12 + q21 * w22), b[3][3] - (q12 * w12 + q22 * w22)
        )
        m11, m12 = -(w11 * t11 + w12 * t12), -(w11 * t12 + w12 * t22)
        m21, m22 = -(w21 * t11 + w22 * t12), -(w21 * t12 + w22 * t22)
        l11, l12 = s11 - (m11 * w11 + m12 * w12), s12 - (m11 * w21 + m12 * w22)
        l22 = s22 - (m21 * w21 + m22 * w22)
        inv = [[l11, l12, m11, m12], [l12, l22, m21, m22], [m11, m21, t11, t12], [m12, m22, t12, t22]]
        p = [(inv[i][0] * r[0] + inv[i][1] * r[1]) + (inv[i][2] * r[2] + inv[i][3] * r[3]) for i in range(4)]
        new = a - ((c[0] * p[0] + c[1] * p[1]) + (c[2] * p[2] + c[3] * p[3]))
        for i in range(4):
            q = (inv[i][0] * c[0] + inv[i][1] * c[1]) + (inv[i][2] * c[2] + inv[i][3] * c[3])
            new = jnp.where(ci == k + i, q, new)
        a_ref[...] = new
        for i in range(4):
            for j in range(4):
                p[i] = jnp.where(lane == k + j, -inv[i][j], p[i])
            a_ref[pl.ds(k + i, 1), :] = p[i]
        return 0

    lax.fori_loop(0, n // 4, step, 0)


def eye(n):
    ri = lax.broadcasted_iota(jnp.int32, (n, n), 0)
    return jnp.where(ri == lax.broadcasted_iota(jnp.int32, (n, n), 1), 1.0, 0.0).astype(F32)


def factor_kernel(sums_ref, out_ref, mat):
    k = sums_ref.shape[0]
    mat[...] = sums_ref[:, -k:] + ridge_factor * eye(k)
    sweep(mat)
    found = jnp.dot(-mat[...], sums_ref[:, :-k], preferred_element_type=F32, precision=HI)
    out_ref[...] = found.astype(BF16)


def hess_kernel(places, near, other, dos_hbm, fac, inverse, proj, mat, dos, sem):
    k = mat.shape[0]
    width = near.shape[2]
    fetch = pltpu.make_async_copy(dos_hbm, dos, sem)
    fetch.start()
    for i in range(8):
        fac[:, pl.ds(pl.multiple_of(places[i] * width, width), width)] = near[i]
        fac[:, pl.ds(pl.multiple_of(places[8 + i] * width, width), width)] = other[i]
    mat[...] = lax.dot_general(fac[...], fac[...], NT, preferred_element_type=F32) + ridge_sample * eye(k)
    sweep(mat)
    inverse[...] = -mat[...]
    fetch.wait()
    total = jnp.dot(fac[...], dos[...], preferred_element_type=F32)
    high = total.astype(BF16)
    proj[:k, :] = high
    proj[k:, :] = (total - high.astype(F32)).astype(BF16)


def finish_kernel(scale, start, genes, places, rows, score, fac, inverse, proj, *rest):
    out, done, sems = rest[-3:]
    cross = lax.dot_general(rows[...], fac[...], NT, preferred_element_type=F32)
    half = jnp.dot(cross, inverse[...], preferred_element_type=F32, precision=HI).astype(BF16)
    coef = jnp.concatenate([half, half], axis=1)
    total = score[...] - jnp.dot(coef, proj[...], preferred_element_type=F32)
    done[...] = (total * scale).astype(BF16)
    copies = [
        pltpu.make_async_copy(
            done.at[pl.ds(i * genes, genes), :], out.at[places[i], 0, pl.ds(start, genes), :], sems.at[i]
        )
        for i in range(rows.shape[0] // genes)
    ]
    for copy in copies:
        copy.start()
    for copy in copies:
        copy.wait()


def finish(places, rows, score, fac, inverse, proj, out, start, genes, panel, samples):
    snps = score.shape[1]
    ins = [rows, score, fac, inverse, proj]
    specs = [pl.BlockSpec(a.shape, lambda n, _, nd=a.ndim: (0,) * nd) for a in ins]
    alias = {}
    if out is not None:
        alias = {len(ins) + 1: 0}
        ins.append(out)
        specs.append(pl.BlockSpec(memory_space=pl.ANY))
    return pl.pallas_call(
        functools.partial(finish_kernel, float(samples) ** -0.5, start, genes),
        out_shape=jax.ShapeDtypeStruct((16, 1, panel, snps), BF16),
        grid_spec=pltpu.PrefetchScalarGridSpec(
            num_scalar_prefetch=1,
            grid=(1,),
            in_specs=specs,
            out_specs=pl.BlockSpec(memory_space=pl.ANY),
            scratch_shapes=[pltpu.VMEM(score.shape, BF16), pltpu.SemaphoreType.DMA((rows.shape[0] // genes,))],
        ),
        input_output_aliases=alias,
        cost_estimate=pl.CostEstimate(
            flops=2 * rows.shape[0] * rows.shape[1] * 256, bytes_accessed=8_000_000, transcendentals=0
        ),
        compiler_params=pltpu.CompilerParams(vmem_limit_bytes=24 << 20),
    )(places, *ins)


def body(expression, loadings, dosage):
    samples, genes = expression.shape
    k = loadings.shape[1]
    n_samp, n_cols = lax.axis_size(SAMP), lax.axis_size(COLS)
    panel = genes // n_samp
    all_samples, snps = dosage.shape
    at = {name: lax.axis_index(name) for name in SAMP + COLS}

    flipped = expression.T
    mine = lax.all_to_all(flipped.reshape(n_samp, panel, samples), SAMP, 0, 0, tiled=True)
    mine = mine.transpose(1, 0, 2).reshape(panel, all_samples)

    both = jnp.concatenate(
        [
            lax.dot_general(loadings, flipped, TN, preferred_element_type=F32),
            lax.dot_general(loadings, loadings, TN, preferred_element_type=F32),
        ],
        axis=1,
    )
    both = lax.all_to_all(both.reshape(n_cols, k // n_cols, samples + k), COLS, 0, 0, tiled=True)
    both = both.sum(axis=0)
    both = lax.all_to_all(jnp.broadcast_to(both[None], (n_cols,) + both.shape), COLS, 0, 0, tiled=True)
    factors = pl.pallas_call(
        factor_kernel,
        out_shape=jax.ShapeDtypeStruct((k, samples), BF16),
        scratch_shapes=[pltpu.VMEM((k, k), F32)],
        cost_estimate=pl.CostEstimate(flops=7_000_000_000, bytes_accessed=400_000, transcendentals=0),
        name="factor",
    )(both.reshape(k, samples + k))

    width = panel // CHUNKS
    groups = []
    for c in range(CHUNKS):
        piece = mine[c * width : c * width + width]
        own = jnp.concatenate([piece] + [cycle(piece, "zl", by) for by in (1, 2, 3)])
        ahead, behind = cycle(own, "y", 1), cycle(own, "y", -1)
        far = cycle(ahead, "y", 1) if c % 2 == 0 else cycle(behind, "y", -1)
        if c < CHUNKS - 1:
            groups.append((c * width, (0, 1, 2, 3), jnp.concatenate([own, ahead, far, behind])))
        else:
            groups.append((c * width, (0, 1, 3), jnp.concatenate([own, ahead, behind])))
            groups.append((c * width, (2,), far))
    scores = [jnp.dot(rows, dosage, preferred_element_type=F32) for _, _, rows in groups]

    two = jnp.stack([factors, cycle(factors, "zh", 1)])
    near = jnp.concatenate([two] + [cycle(two, "x", by) for by in (1, 2, 3)])
    other = cycle(near, "core", 1)
    back = jnp.arange(16)
    from_core = (at["core"] - back // 8) % 2
    from_x = (at["x"] - back // 2 % 4) % 4
    from_zh = (at["zh"] - back % 2) % 2
    order = (from_zh * 8 + from_x * 2 + from_core).astype(jnp.int32)
    fac, inverse, proj = pl.pallas_call(
        hess_kernel,
        out_shape=(
            jax.ShapeDtypeStruct((k, all_samples), BF16),
            jax.ShapeDtypeStruct((k, k), F32),
            jax.ShapeDtypeStruct((2 * k, snps), BF16),
        ),
        in_specs=[
            pl.BlockSpec(memory_space=pltpu.SMEM),
            pl.BlockSpec(memory_space=pltpu.VMEM),
            pl.BlockSpec(memory_space=pltpu.VMEM),
            pl.BlockSpec(memory_space=pl.ANY),
        ],
        scratch_shapes=[
            pltpu.VMEM((k, k), F32),
            pltpu.VMEM(dosage.shape, BF16),
            pltpu.SemaphoreType.DMA,
        ],
        cost_estimate=pl.CostEstimate(flops=9_000_000_000, bytes_accessed=10_000_000, transcendentals=0),
        compiler_params=pltpu.CompilerParams(vmem_limit_bytes=24 << 20),
        name="hess",
    )(order, near, other, dosage)

    back_z = (at["zl"] - jnp.arange(4)) % 4
    back_y = (at["y"] - jnp.arange(4)) % 4
    places = (back_z[None, :] * 4 + back_y[:, None]).astype(jnp.int32)
    out = None
    for (start, slots, rows), score in zip(groups, scores):
        where = jnp.concatenate([places[m] for m in slots])
        out = finish(where, rows, score, fac, inverse, proj, out, start, width, panel, all_samples)
    return out


def solution(mesh):
    fine = Mesh(mesh.devices.reshape(2, 4, 2, 4, 4), SAMP + COLS)
    placed = (P(SAMP, COLS), P(COLS, None), P(None, COLS))
    return jax.shard_map(body, mesh=fine, in_specs=placed, out_specs=P(None, SAMP, None, COLS), check_vma=False)
```

```python
import functools

import jax
import jax.numpy as jnp
from jax import lax
from jax.experimental import pallas as pl
from jax.experimental.pallas import tpu as pltpu
from jax.sharding import Mesh, PartitionSpec as P

ridge_factor = 1.0
ridge_sample = 1.0
SAMP = ("zh", "x", "core")
COLS = ("zl", "y")
CHUNKS = 2
F32 = jnp.float32
BF16 = jnp.bfloat16
HI = lax.Precision.HIGHEST
NT = (((1,), (1,)), ((), ()))
TN = (((0,), (0,)), ((), ()))


def cycle(array, axis, by):
    size = lax.axis_size(axis)
    return lax.ppermute(array, axis, [(i, (i + by) % size) for i in range(size)])


def invert2(a, b, c):
    r = 1.0 / (a * c - b * b)
    return c * r, -b * r, a * r


def sweep(a_ref):
    n = a_ref.shape[0]
    ci = lax.broadcasted_iota(jnp.int32, (n, n), 1)
    lane = ci[:1]

    def step(t, _):
        k = 4 * t
        a = a_ref[...]
        r = [a_ref[pl.ds(k + i, 1), :] for i in range(4)]
        c = [jnp.sum(jnp.where(ci == k + i, a, 0.0), axis=1, keepdims=True) for i in range(4)]
        b = [[None] * i + [jnp.sum(jnp.where(lane == k + j, r[i], 0.0), axis=1, keepdims=True) for j in range(i, 4)] for i in range(4)]
        s11, s12, s22 = invert2(b[0][0], b[0][1], b[1][1])
        q11, q12, q21, q22 = b[0][2], b[0][3], b[1][2], b[1][3]
        w11, w12 = s11 * q11 + s12 * q21, s11 * q12 + s12 * q22
        w21, w22 = s12 * q11 + s22 * q21, s12 * q12 + s22 * q22
        t11, t12, t22 = invert2(
            b[2][2] - (q11 * w11 + q21 * w21), b[2][3] - (q11 * w12 + q21 * w22), b[3][3] - (q12 * w12 + q22 * w22)
        )
        m11, m12 = -(w11 * t11 + w12 * t12), -(w11 * t12 + w12 * t22)
        m21, m22 = -(w21 * t11 + w22 * t12), -(w21 * t12 + w22 * t22)
        l11, l12 = s11 - (m11 * w11 + m12 * w12), s12 - (m11 * w21 + m12 * w22)
        l22 = s22 - (m21 * w21 + m22 * w22)
        inv = [[l11, l12, m11, m12], [l12, l22, m21, m22], [m11, m21, t11, t12], [m12, m22, t12, t22]]
        p = [(inv[i][0] * r[0] + inv[i][1] * r[1]) + (inv[i][2] * r[2] + inv[i][3] * r[3]) for i in range(4)]
        new = a - ((c[0] * p[0] + c[1] * p[1]) + (c[2] * p[2] + c[3] * p[3]))
        for i in range(4):
            q = (inv[i][0] * c[0] + inv[i][1] * c[1]) + (inv[i][2] * c[2] + inv[i][3] * c[3])
            new = jnp.where(ci == k + i, q, new)
        a_ref[...] = new
        for i in range(4):
            for j in range(4):
                p[i] = jnp.where(lane == k + j, -inv[i][j], p[i])
            a_ref[pl.ds(k + i, 1), :] = p[i]
        return 0

    lax.fori_loop(0, n // 4, step, 0)


def eye(n):
    ri = lax.broadcasted_iota(jnp.int32, (n, n), 0)
    return jnp.where(ri == lax.broadcasted_iota(jnp.int32, (n, n), 1), 1.0, 0.0).astype(F32)


def factor_kernel(sums_ref, out_ref, mat):
    k = sums_ref.shape[0]
    mat[...] = sums_ref[:, -k:] + ridge_factor * eye(k)
    sweep(mat)
    found = jnp.dot(-mat[...], sums_ref[:, :-k], preferred_element_type=F32, precision=HI)
    out_ref[...] = found.astype(BF16)


def hess_kernel(places, near, other, dos_hbm, fac, inverse, proj, mat, dos, sem):
    k = mat.shape[0]
    width = near.shape[2]
    fetch = pltpu.make_async_copy(dos_hbm, dos, sem)
    fetch.start()
    for i in range(8):
        fac[:, pl.ds(pl.multiple_of(places[i] * width, width), width)] = near[i]
        fac[:, pl.ds(pl.multiple_of(places[8 + i] * width, width), width)] = other[i]
    mat[...] = lax.dot_general(fac[...], fac[...], NT, preferred_element_type=F32) + ridge_sample * eye(k)
    sweep(mat)
    inverse[...] = -mat[...]
    fetch.wait()
    total = jnp.dot(fac[...], dos[...], preferred_element_type=F32)
    high = total.astype(BF16)
    proj[:k, :] = high
    proj[k:, :] = (total - high.astype(F32)).astype(BF16)


def finish_kernel(scale, start, genes, count, places, *refs):
    pieces, scores = refs[:count], refs[count : 2 * count]
    fac, inverse, proj = refs[2 * count : 2 * count + 3]
    out, done, sems = refs[-3:]
    cross = [lax.dot_general(piece[...], fac[...], NT, preferred_element_type=F32) for piece in pieces]
    cross = jnp.concatenate(cross)
    half = jnp.dot(cross, inverse[...], preferred_element_type=F32, precision=HI).astype(BF16)
    coef = jnp.concatenate([half, half], axis=1)
    at, copies = 0, []
    for score in scores:
        rows = score.shape[0]
        total = score[...] - jnp.dot(coef[at : at + rows], proj[...], preferred_element_type=F32)
        done[pl.ds(at, rows), :] = (total * scale).astype(BF16)
        for i in range(at // genes, (at + rows) // genes):
            copy = pltpu.make_async_copy(
                done.at[pl.ds(i * genes, genes), :], out.at[places[i], 0, pl.ds(start, genes), :], sems.at[i]
            )
            copy.start()
            copies.append(copy)
        at += rows
    for copy in copies:
        copy.wait()


def finish(places, pieces, scores, fac, inverse, proj, out, start, genes, panel, samples):
    snps = scores[0].shape[1]
    rows = sum(p.shape[0] for p in pieces)
    ins = list(pieces) + list(scores) + [fac, inverse, proj]
    specs = [pl.BlockSpec(a.shape, lambda n, _, nd=a.ndim: (0,) * nd) for a in ins]
    alias = {}
    if out is not None:
        alias = {len(ins) + 1: 0}
        ins.append(out)
        specs.append(pl.BlockSpec(memory_space=pl.ANY))
    return pl.pallas_call(
        functools.partial(finish_kernel, float(samples) ** -0.5, start, genes, len(pieces)),
        out_shape=jax.ShapeDtypeStruct((16, 1, panel, snps), BF16),
        grid_spec=pltpu.PrefetchScalarGridSpec(
            num_scalar_prefetch=1,
            grid=(1,),
            in_specs=specs,
            out_specs=pl.BlockSpec(memory_space=pl.ANY),
            scratch_shapes=[pltpu.VMEM((rows, snps), BF16), pltpu.SemaphoreType.DMA((rows // genes,))],
        ),
        input_output_aliases=alias,
        cost_estimate=pl.CostEstimate(flops=2 * rows * samples * 256, bytes_accessed=rows * 16384, transcendentals=0),
        compiler_params=pltpu.CompilerParams(vmem_limit_bytes=30 << 20),
    )(places, *ins)


def body(expression, loadings, dosage):
    samples, genes = expression.shape
    k = loadings.shape[1]
    n_samp, n_cols = lax.axis_size(SAMP), lax.axis_size(COLS)
    panel = genes // n_samp
    all_samples, snps = dosage.shape
    at = {name: lax.axis_index(name) for name in SAMP + COLS}

    flipped = expression.T
    mine = lax.all_to_all(flipped.reshape(n_samp, panel, samples), SAMP, 0, 0, tiled=True)
    mine = mine.transpose(1, 0, 2).reshape(panel, all_samples)

    both = jnp.concatenate(
        [
            lax.dot_general(loadings, flipped, TN, preferred_element_type=F32),
            lax.dot_general(loadings, loadings, TN, preferred_element_type=F32),
        ],
        axis=1,
    )
    both = lax.all_to_all(both.reshape(n_cols, k // n_cols, samples + k), COLS, 0, 0, tiled=True)
    both = both.sum(axis=0)
    both = lax.all_to_all(jnp.broadcast_to(both[None], (n_cols,) + both.shape), COLS, 0, 0, tiled=True)
    factors = pl.pallas_call(
        factor_kernel,
        out_shape=jax.ShapeDtypeStruct((k, samples), BF16),
        scratch_shapes=[pltpu.VMEM((k, k), F32)],
        cost_estimate=pl.CostEstimate(flops=7_000_000_000, bytes_accessed=400_000, transcendentals=0),
        name="factor",
    )(both.reshape(k, samples + k))

    width = panel // CHUNKS
    groups = []
    for c in range(CHUNKS):
        piece = mine[c * width : c * width + width]
        own = jnp.concatenate([piece] + [cycle(piece, "zl", by) for by in (1, 2, 3)])
        ahead, behind = cycle(own, "y", 1), cycle(own, "y", -1)
        low, high = cycle(ahead[: 2 * width], "y", 1), cycle(behind[2 * width :], "y", -1)
        near_slots, far_slots = [(0, 4), (4, 8), (12, 16)], [(8, 10), (10, 12)]
        if c < CHUNKS - 1:
            groups.append((c * width, near_slots + far_slots, [own, ahead, behind, low, high]))
        else:
            groups.append((c * width, near_slots, [own, ahead, behind]))
            groups.append((c * width, far_slots, [low, high]))
    scores = [[jnp.dot(rows, dosage, preferred_element_type=F32) for rows in pieces] for _, _, pieces in groups]

    two = jnp.stack([factors, cycle(factors, "zh", 1)])
    near = jnp.concatenate([two] + [cycle(two, "x", by) for by in (1, 2, 3)])
    other = cycle(near, "core", 1)
    back = jnp.arange(16)
    from_core = (at["core"] - back // 8) % 2
    from_x = (at["x"] - back // 2 % 4) % 4
    from_zh = (at["zh"] - back % 2) % 2
    order = (from_zh * 8 + from_x * 2 + from_core).astype(jnp.int32)
    fac, inverse, proj = pl.pallas_call(
        hess_kernel,
        out_shape=(
            jax.ShapeDtypeStruct((k, all_samples), BF16),
            jax.ShapeDtypeStruct((k, k), F32),
            jax.ShapeDtypeStruct((2 * k, snps), BF16),
        ),
        in_specs=[
            pl.BlockSpec(memory_space=pltpu.SMEM),
            pl.BlockSpec(memory_space=pltpu.VMEM),
            pl.BlockSpec(memory_space=pltpu.VMEM),
            pl.BlockSpec(memory_space=pl.ANY),
        ],
        scratch_shapes=[
            pltpu.VMEM((k, k), F32),
            pltpu.VMEM(dosage.shape, BF16),
            pltpu.SemaphoreType.DMA,
        ],
        cost_estimate=pl.CostEstimate(flops=9_000_000_000, bytes_accessed=10_000_000, transcendentals=0),
        compiler_params=pltpu.CompilerParams(vmem_limit_bytes=24 << 20),
        name="hess",
    )(order, near, other, dosage)

    back_z = (at["zl"] - jnp.arange(4)) % 4
    back_y = (at["y"] - jnp.arange(4)) % 4
    places = (back_z[None, :] * 4 + back_y[:, None]).astype(jnp.int32).reshape(16)
    out = None
    for (start, slots, pieces), score in zip(groups, scores):
        where = jnp.concatenate([places[a:b] for a, b in slots])
        out = finish(where, pieces, score, fac, inverse, proj, out, start, width, panel, all_samples)
    return out


def solution(mesh):
    fine = Mesh(mesh.devices.reshape(2, 4, 2, 4, 4), SAMP + COLS)
    placed = (P(SAMP, COLS), P(COLS, None), P(None, COLS))
    return jax.shard_map(body, mesh=fine, in_specs=placed, out_specs=P(None, SAMP, None, COLS), check_vma=False)
```

```python
import functools

import jax
import jax.numpy as jnp
from jax import lax
from jax.experimental import pallas as pl
from jax.experimental.pallas import tpu as pltpu
from jax.sharding import Mesh, PartitionSpec as P

ridge_factor = 1.0
ridge_sample = 1.0
SAMP = ("zh", "x", "core")
COLS = ("zl", "y")
CHUNKS = 2
F32 = jnp.float32
BF16 = jnp.bfloat16
HI = lax.Precision.HIGHEST
NT = (((1,), (1,)), ((), ()))
TN = (((0,), (0,)), ((), ()))


def cycle(array, axis, by):
    size = lax.axis_size(axis)
    return lax.ppermute(array, axis, [(i, (i + by) % size) for i in range(size)])


def invert2(a, b, c):
    r = 1.0 / (a * c - b * b)
    return c * r, -b * r, a * r


def sweep(a_ref):
    n = a_ref.shape[0]
    ci = lax.broadcasted_iota(jnp.int32, (n, n), 1)
    lane = ci[:1]

    def step(t, _):
        k = 4 * t
        a = a_ref[...]
        r = [a_ref[pl.ds(k + i, 1), :] for i in range(4)]
        c = [jnp.sum(jnp.where(ci == k + i, a, 0.0), axis=1, keepdims=True) for i in range(4)]
        b = [[None] * i + [jnp.sum(jnp.where(lane == k + j, r[i], 0.0), axis=1, keepdims=True) for j in range(i, 4)] for i in range(4)]
        s11, s12, s22 = invert2(b[0][0], b[0][1], b[1][1])
        q11, q12, q21, q22 = b[0][2], b[0][3], b[1][2], b[1][3]
        w11, w12 = s11 * q11 + s12 * q21, s11 * q12 + s12 * q22
        w21, w22 = s12 * q11 + s22 * q21, s12 * q12 + s22 * q22
        t11, t12, t22 = invert2(
            b[2][2] - (q11 * w11 + q21 * w21), b[2][3] - (q11 * w12 + q21 * w22), b[3][3] - (q12 * w12 + q22 * w22)
        )
        m11, m12 = -(w11 * t11 + w12 * t12), -(w11 * t12 + w12 * t22)
        m21, m22 = -(w21 * t11 + w22 * t12), -(w21 * t12 + w22 * t22)
        l11, l12 = s11 - (m11 * w11 + m12 * w12), s12 - (m11 * w21 + m12 * w22)
        l22 = s22 - (m21 * w21 + m22 * w22)
        inv = [[l11, l12, m11, m12], [l12, l22, m21, m22], [m11, m21, t11, t12], [m12, m22, t12, t22]]
        p = [(inv[i][0] * r[0] + inv[i][1] * r[1]) + (inv[i][2] * r[2] + inv[i][3] * r[3]) for i in range(4)]
        new = a - ((c[0] * p[0] + c[1] * p[1]) + (c[2] * p[2] + c[3] * p[3]))
        for i in range(4):
            q = (inv[i][0] * c[0] + inv[i][1] * c[1]) + (inv[i][2] * c[2] + inv[i][3] * c[3])
            new = jnp.where(ci == k + i, q, new)
        a_ref[...] = new
        for i in range(4):
            for j in range(4):
                p[i] = jnp.where(lane == k + j, -inv[i][j], p[i])
            a_ref[pl.ds(k + i, 1), :] = p[i]
        return 0

    lax.fori_loop(0, n // 4, step, 0)


def eye(n):
    ri = lax.broadcasted_iota(jnp.int32, (n, n), 0)
    return jnp.where(ri == lax.broadcasted_iota(jnp.int32, (n, n), 1), 1.0, 0.0).astype(F32)


def factor_kernel(sums_ref, out_ref, mat):
    k = sums_ref.shape[0]
    mat[...] = sums_ref[:, -k:] + ridge_factor * eye(k)
    sweep(mat)
    found = jnp.dot(-mat[...], sums_ref[:, :-k], preferred_element_type=F32, precision=HI)
    out_ref[...] = found.astype(BF16)


def hess_kernel(places, near, other, dos_hbm, fac, inverse, proj, mat, dos, sem):
    k = mat.shape[0]
    width = near.shape[2]
    fetch = pltpu.make_async_copy(dos_hbm, dos, sem)
    fetch.start()
    for i in range(8):
        fac[:, pl.ds(pl.multiple_of(places[i] * width, width), width)] = near[i]
        fac[:, pl.ds(pl.multiple_of(places[8 + i] * width, width), width)] = other[i]
    mat[...] = lax.dot_general(fac[...], fac[...], NT, preferred_element_type=F32) + ridge_sample * eye(k)
    sweep(mat)
    inverse[...] = -mat[...]
    fetch.wait()
    total = jnp.dot(fac[...], dos[...], preferred_element_type=F32)
    high = total.astype(BF16)
    proj[:k, :] = high
    proj[k:, :] = (total - high.astype(F32)).astype(BF16)


def finish_kernel(scale, start, genes, count, places, *refs):
    pieces, scores = refs[:count], refs[count : 2 * count]
    fac, inverse, proj = refs[2 * count : 2 * count + 3]
    out, done, sems = refs[-3:]
    cross = [lax.dot_general(piece[...], fac[...], NT, preferred_element_type=F32) for piece in pieces]
    cross = jnp.concatenate(cross)
    half = jnp.dot(cross, inverse[...], preferred_element_type=F32, precision=HI).astype(BF16)
    coef = jnp.concatenate([half, half], axis=1)
    at, copies = 0, []
    for score in scores:
        rows = score.shape[0]
        total = score[...] - jnp.dot(coef[at : at + rows], proj[...], preferred_element_type=F32)
        done[pl.ds(at, rows), :] = (total * scale).astype(BF16)
        for i in range(at // genes, (at + rows) // genes):
            copy = pltpu.make_async_copy(
                done.at[pl.ds(i * genes, genes), :], out.at[places[i], 0, pl.ds(start, genes), :], sems.at[i]
            )
            copy.start()
            copies.append(copy)
        at += rows
    for copy in copies:
        copy.wait()


def finish(places, pieces, scores, fac, inverse, proj, out, start, genes, panel, samples):
    snps = scores[0].shape[1]
    rows = sum(p.shape[0] for p in pieces)
    ins = list(pieces) + list(scores) + [fac, inverse, proj]
    specs = [pl.BlockSpec(a.shape, lambda n, _, nd=a.ndim: (0,) * nd) for a in ins]
    alias = {}
    if out is not None:
        alias = {len(ins) + 1: 0}
        ins.append(out)
        specs.append(pl.BlockSpec(memory_space=pl.ANY))
    return pl.pallas_call(
        functools.partial(finish_kernel, float(samples) ** -0.5, start, genes, len(pieces)),
        out_shape=jax.ShapeDtypeStruct((16, 1, panel, snps), BF16),
        grid_spec=pltpu.PrefetchScalarGridSpec(
            num_scalar_prefetch=1,
            grid=(1,),
            in_specs=specs,
            out_specs=pl.BlockSpec(memory_space=pl.ANY),
            scratch_shapes=[pltpu.VMEM((rows, snps), BF16), pltpu.SemaphoreType.DMA((rows // genes,))],
        ),
        input_output_aliases=alias,
        cost_estimate=pl.CostEstimate(flops=2 * rows * samples * 256, bytes_accessed=rows * 16384, transcendentals=0),
        compiler_params=pltpu.CompilerParams(vmem_limit_bytes=30 << 20),
    )(places, *ins)


def body(expression, loadings, dosage):
    samples, genes = expression.shape
    k = loadings.shape[1]
    n_samp, n_cols = lax.axis_size(SAMP), lax.axis_size(COLS)
    panel = genes // n_samp
    all_samples, snps = dosage.shape
    at = {name: lax.axis_index(name) for name in SAMP + COLS}

    flipped = expression.T
    mine = lax.all_to_all(flipped.reshape(n_samp, panel, samples), SAMP, 0, 0, tiled=True)
    mine = mine.transpose(1, 0, 2).reshape(panel, all_samples)

    both = jnp.concatenate(
        [
            lax.dot_general(loadings, flipped, TN, preferred_element_type=F32),
            lax.dot_general(loadings, loadings, TN, preferred_element_type=F32),
        ],
        axis=1,
    )
    both = lax.all_to_all(both.reshape(n_cols, k // n_cols, samples + k), COLS, 0, 0, tiled=True)
    both = both.sum(axis=0)
    both = lax.all_to_all(jnp.broadcast_to(both[None], (n_cols,) + both.shape), COLS, 0, 0, tiled=True)
    factors = pl.pallas_call(
        factor_kernel,
        out_shape=jax.ShapeDtypeStruct((k, samples), BF16),
        scratch_shapes=[pltpu.VMEM((k, k), F32)],
        cost_estimate=pl.CostEstimate(flops=7_000_000_000, bytes_accessed=400_000, transcendentals=0),
        name="factor",
    )(both.reshape(k, samples + k))

    width = panel // CHUNKS
    groups = []
    for c in range(CHUNKS):
        piece = mine[c * width : c * width + width]
        own = jnp.concatenate([piece] + [cycle(piece, "zl", by) for by in (1, 2, 3)])
        ahead, behind = cycle(own, "y", 1), cycle(own, "y", -1)
        low, high = ahead[: 2 * width], behind[2 * width :]
        low, high = cycle(low, "y", 1), cycle(high, "y", -1)
        near_slots, far_slots = [(0, 4), (4, 8), (12, 16)], [(8, 10), (10, 12)]
        if c < CHUNKS - 1:
            groups.append((c * width, near_slots + far_slots, [own, ahead, behind, low, high]))
        else:
            groups.append((c * width, near_slots, [own, ahead, behind]))
            groups.append((c * width, far_slots, [low, high]))
    scores = []
    for _, _, pieces in groups:
        scores.append([])
        for rows in pieces:
            scores[-1].append(jnp.dot(rows, dosage, preferred_element_type=F32))

    two = jnp.stack([factors, cycle(factors, "zh", 1)])
    near = jnp.concatenate([two] + [cycle(two, "x", by) for by in (1, 2, 3)])
    other = cycle(near, "core", 1)
    back = jnp.arange(16)
    from_core = (at["core"] - back // 8) % 2
    from_x = (at["x"] - back // 2 % 4) % 4
    from_zh = (at["zh"] - back % 2) % 2
    order = (from_zh * 8 + from_x * 2 + from_core).astype(jnp.int32)
    fac, inverse, proj = pl.pallas_call(
        hess_kernel,
        out_shape=(
            jax.ShapeDtypeStruct((k, all_samples), BF16),
            jax.ShapeDtypeStruct((k, k), F32),
            jax.ShapeDtypeStruct((2 * k, snps), BF16),
        ),
        in_specs=[
            pl.BlockSpec(memory_space=pltpu.SMEM),
            pl.BlockSpec(memory_space=pltpu.VMEM),
            pl.BlockSpec(memory_space=pltpu.VMEM),
            pl.BlockSpec(memory_space=pl.ANY),
        ],
        scratch_shapes=[
            pltpu.VMEM((k, k), F32),
            pltpu.VMEM(dosage.shape, BF16),
            pltpu.SemaphoreType.DMA,
        ],
        cost_estimate=pl.CostEstimate(flops=9_000_000_000, bytes_accessed=10_000_000, transcendentals=0),
        compiler_params=pltpu.CompilerParams(vmem_limit_bytes=24 << 20),
        name="hess",
    )(order, near, other, dosage)

    back_z = (at["zl"] - jnp.arange(4)) % 4
    back_y = (at["y"] - jnp.arange(4)) % 4
    places = (back_z[None, :] * 4 + back_y[:, None]).astype(jnp.int32).reshape(16)
    out = None
    for (start, slots, pieces), score in zip(groups, scores):
        where = jnp.concatenate([places[a:b] for a, b in slots])
        out = finish(where, pieces, score, fac, inverse, proj, out, start, width, panel, all_samples)
    return out


def solution(mesh):
    fine = Mesh(mesh.devices.reshape(2, 4, 2, 4, 4), SAMP + COLS)
    placed = (P(SAMP, COLS), P(COLS, None), P(None, COLS))
    return jax.shard_map(body, mesh=fine, in_specs=placed, out_specs=P(None, SAMP, None, COLS), check_vma=False)
```

```python
import functools

import jax
import jax.numpy as jnp
from jax import lax
from jax.experimental import pallas as pl
from jax.experimental.pallas import tpu as pltpu
from jax.sharding import Mesh, PartitionSpec as P

ridge_factor = 1.0
ridge_sample = 1.0
SAMP = ("zh", "x", "core")
COLS = ("zl", "y")
CHUNKS = 2
F32 = jnp.float32
BF16 = jnp.bfloat16
HI = lax.Precision.HIGHEST
NT = (((1,), (1,)), ((), ()))
TN = (((0,), (0,)), ((), ()))


def cycle(array, axis, by):
    size = lax.axis_size(axis)
    return lax.ppermute(array, axis, [(i, (i + by) % size) for i in range(size)])


def invert2(a, b, c):
    r = 1.0 / (a * c - b * b)
    return c * r, -b * r, a * r


def sweep(a_ref, beside):
    n = a_ref.shape[0]
    ci = lax.broadcasted_iota(jnp.int32, (n, n), 1)
    lane = ci[:1]

    def step(t, _):
        k = 4 * t
        beside(t, True)
        a = a_ref[...]
        r = [a_ref[pl.ds(k + i, 1), :] for i in range(4)]
        c = [jnp.sum(jnp.where(ci == k + i, a, 0.0), axis=1, keepdims=True) for i in range(4)]
        b = [[None] * i + [jnp.sum(jnp.where(lane == k + j, r[i], 0.0), axis=1, keepdims=True) for j in range(i, 4)] for i in range(4)]
        s11, s12, s22 = invert2(b[0][0], b[0][1], b[1][1])
        q11, q12, q21, q22 = b[0][2], b[0][3], b[1][2], b[1][3]
        w11, w12 = s11 * q11 + s12 * q21, s11 * q12 + s12 * q22
        w21, w22 = s12 * q11 + s22 * q21, s12 * q12 + s22 * q22
        t11, t12, t22 = invert2(
            b[2][2] - (q11 * w11 + q21 * w21), b[2][3] - (q11 * w12 + q21 * w22), b[3][3] - (q12 * w12 + q22 * w22)
        )
        m11, m12 = -(w11 * t11 + w12 * t12), -(w11 * t12 + w12 * t22)
        m21, m22 = -(w21 * t11 + w22 * t12), -(w21 * t12 + w22 * t22)
        l11, l12 = s11 - (m11 * w11 + m12 * w12), s12 - (m11 * w21 + m12 * w22)
        l22 = s22 - (m21 * w21 + m22 * w22)
        inv = [[l11, l12, m11, m12], [l12, l22, m21, m22], [m11, m21, t11, t12], [m12, m22, t12, t22]]
        p = [(inv[i][0] * r[0] + inv[i][1] * r[1]) + (inv[i][2] * r[2] + inv[i][3] * r[3]) for i in range(4)]
        new = a - ((c[0] * p[0] + c[1] * p[1]) + (c[2] * p[2] + c[3] * p[3]))
        for i in range(4):
            q = (inv[i][0] * c[0] + inv[i][1] * c[1]) + (inv[i][2] * c[2] + inv[i][3] * c[3])
            new = jnp.where(ci == k + i, q, new)
        a_ref[...] = new
        for i in range(4):
            for j in range(4):
                p[i] = jnp.where(lane == k + j, -inv[i][j], p[i])
            a_ref[pl.ds(k + i, 1), :] = p[i]
        beside(t)
        return 0

    lax.fori_loop(0, n // 4, step, 0)


def eye(n):
    ri = lax.broadcasted_iota(jnp.int32, (n, n), 0)
    return jnp.where(ri == lax.broadcasted_iota(jnp.int32, (n, n), 1), 1.0, 0.0).astype(F32)


STEPS = 32
TILE = 256


class Products:
    def __init__(self, dos_hbm, dos, sems):
        self.dos = dos
        self.copies = [
            pltpu.make_async_copy(
                dos_hbm.at[:, pl.ds(n * TILE, TILE)], dos.at[:, pl.ds(n * TILE, TILE)], sems.at[n]
            )
            for n in range(dos.shape[1] // TILE)
        ]
        self.shares = STEPS // len(self.copies)
        self.pairs = []
        for copy in self.copies:
            copy.start()

    def __call__(self, t, before=False):
        if before:
            for n, copy in enumerate(self.copies):
                pl.when(t == n * self.shares)(copy.wait)
            return
        depth = self.dos.shape[0] // self.shares
        part = lax.rem(t, self.shares)
        inner = pl.ds(pl.multiple_of(part * depth, depth), depth)
        column = pl.ds(pl.multiple_of(lax.div(t, self.shares) * TILE, TILE), TILE)
        tile = self.dos[inner, column]
        for rows, out in self.pairs:
            found = jnp.dot(rows[:, inner], tile, preferred_element_type=F32)
            out[:, column] = jnp.where(part == 0, found, out[:, column] + found)


def factor_kernel(sums_ref, rows, dos_hbm, out_ref, score, mat, dos, sems):
    k = sums_ref.shape[0]
    products = Products(dos_hbm, dos, sems)
    products.pairs = [(rows, score)]
    mat[...] = sums_ref[:, -k:] + ridge_factor * eye(k)
    sweep(mat, products)
    found = jnp.dot(-mat[...], sums_ref[:, :-k], preferred_element_type=F32, precision=HI)
    out_ref[...] = found.astype(BF16)


def hess_kernel(places, near, other, ahead, behind, dos_hbm, fac, inverse, proj, score1, score2, mat, total, dos, sems):
    k = mat.shape[0]
    width = near.shape[2]
    products = Products(dos_hbm, dos, sems)
    products.pairs = [(fac, total), (ahead, score1), (behind, score2)]
    for i in range(8):
        fac[:, pl.ds(pl.multiple_of(places[i] * width, width), width)] = near[i]
        fac[:, pl.ds(pl.multiple_of(places[8 + i] * width, width), width)] = other[i]
    mat[...] = lax.dot_general(fac[...], fac[...], NT, preferred_element_type=F32) + ridge_sample * eye(k)
    sweep(mat, products)
    inverse[...] = -mat[...]
    found = total[...]
    high = found.astype(BF16)
    proj[:k, :] = high
    proj[k:, :] = (found - high.astype(F32)).astype(BF16)


def finish_kernel(scale, genes, spots, given, places, *refs):
    count = len(spots)
    pieces, scores = refs[:count], refs[count : count + given]
    dos, fac, inverse, proj = refs[count + given : count + given + 4]
    out, done, coef, sems = refs[-4:]
    n = pl.program_id(0)

    @pl.when(n == 0)
    def _():
        at = 0
        for piece in pieces:
            cross = lax.dot_general(piece[...], fac[...], NT, preferred_element_type=F32)
            half = jnp.dot(cross, inverse[...], preferred_element_type=F32, precision=HI).astype(BF16)
            coef[pl.ds(at, piece.shape[0]), :] = jnp.concatenate([half, half], axis=1)
            at += piece.shape[0]

    at = 0
    for i, piece in enumerate(pieces):
        rows = pl.ds(at, piece.shape[0])
        total = scores[i][...] if i < given else jnp.dot(piece[...], dos[...], preferred_element_type=F32)
        total -= jnp.dot(coef[rows, :], proj[...], preferred_element_type=F32)
        done[rows, pl.ds(pl.multiple_of(n * TILE, TILE), TILE)] = (total * scale).astype(BF16)
        at += piece.shape[0]

    @pl.when(n == pl.num_programs(0) - 1)
    def _():
        copies, at = [], 0
        for (start, slot), piece in zip(spots, pieces):
            for i in range(piece.shape[0] // genes):
                copies.append(
                    pltpu.make_async_copy(
                        done.at[pl.ds(at, genes), :],
                        out.at[places[slot + i], 0, pl.ds(start, genes), :],
                        sems.at[at // genes],
                    )
                )
                at += genes
        for copy in copies:
            copy.start()
        for copy in copies:
            copy.wait()


def finish(places, spots, pieces, scores, dosage, fac, inverse, proj, out, genes, panel):
    samples, snps = dosage.shape
    rows = sum(p.shape[0] for p in pieces)
    fixed = lambda a: pl.BlockSpec(a.shape, lambda n, _: (0, 0), pipeline_mode=pl.Buffered(1))
    across = lambda a: pl.BlockSpec((a.shape[0], TILE), lambda n, _: (0, n))
    ins = list(pieces) + list(scores) + [dosage, fac, inverse, proj]
    specs = [fixed(a) for a in pieces] + [across(a) for a in scores]
    specs += [across(dosage), fixed(fac), fixed(inverse), across(proj)]
    alias = {}
    if out is not None:
        alias = {len(ins) + 1: 0}
        ins.append(out)
        specs.append(pl.BlockSpec(memory_space=pl.ANY))
    return pl.pallas_call(
        functools.partial(finish_kernel, float(samples) ** -0.5, genes, spots, len(scores)),
        out_shape=jax.ShapeDtypeStruct((16, 1, panel, snps), BF16),
        grid_spec=pltpu.PrefetchScalarGridSpec(
            num_scalar_prefetch=1,
            grid=(snps // TILE,),
            in_specs=specs,
            out_specs=pl.BlockSpec(memory_space=pl.ANY),
            scratch_shapes=[
                pltpu.VMEM((rows, snps), BF16),
                pltpu.VMEM((rows, proj.shape[0]), BF16),
                pltpu.SemaphoreType.DMA((rows // genes,)),
            ],
        ),
        input_output_aliases=alias,
        cost_estimate=pl.CostEstimate(flops=2 * rows * samples * 1024, bytes_accessed=rows * 16384, transcendentals=0),
        compiler_params=pltpu.CompilerParams(vmem_limit_bytes=36 << 20),
    )(places, *ins)


def body(expression, loadings, dosage):
    samples, genes = expression.shape
    k = loadings.shape[1]
    n_samp, n_cols = lax.axis_size(SAMP), lax.axis_size(COLS)
    panel = genes // n_samp
    all_samples, snps = dosage.shape
    at = {name: lax.axis_index(name) for name in SAMP + COLS}

    flipped = expression.T
    mine = lax.all_to_all(flipped.reshape(n_samp, panel, samples), SAMP, 0, 0, tiled=True)
    mine = mine.transpose(1, 0, 2).reshape(panel, all_samples)

    both = jnp.concatenate(
        [
            lax.dot_general(loadings, flipped, TN, preferred_element_type=F32),
            lax.dot_general(loadings, loadings, TN, preferred_element_type=F32),
        ],
        axis=1,
    )
    both = lax.all_to_all(both.reshape(n_cols, k // n_cols, samples + k), COLS, 0, 0, tiled=True)
    both = both.sum(axis=0)
    both = lax.all_to_all(jnp.broadcast_to(both[None], (n_cols,) + both.shape), COLS, 0, 0, tiled=True)
    width = panel // CHUNKS
    groups = []
    for c in range(CHUNKS):
        piece = mine[c * width : c * width + width]
        own = jnp.concatenate([piece] + [cycle(piece, "zl", by) for by in (1, 2, 3)])
        ahead, behind = cycle(own, "y", 1), cycle(own, "y", -1)
        low, high = ahead[: 2 * width], behind[2 * width :]
        low, high = cycle(low, "y", 1), cycle(high, "y", -1)
        groups.append((own, ahead, behind, low, high))

    vmem, hbm = pl.BlockSpec(memory_space=pltpu.VMEM), pl.BlockSpec(memory_space=pltpu.HBM)
    table = jax.ShapeDtypeStruct((4 * width, snps), F32)
    tiles = [pltpu.VMEM(dosage.shape, BF16), pltpu.SemaphoreType.DMA((snps // TILE,))]
    roomy = pltpu.CompilerParams(vmem_limit_bytes=30 << 20)
    factors, score0 = pl.pallas_call(
        factor_kernel,
        out_shape=(jax.ShapeDtypeStruct((k, samples), BF16), table),
        in_specs=[vmem, vmem, hbm],
        scratch_shapes=[pltpu.VMEM((k, k), F32)] + tiles,
        cost_estimate=pl.CostEstimate(flops=7_000_000_000, bytes_accessed=400_000, transcendentals=0),
        compiler_params=roomy,
        name="factor",
    )(both.reshape(k, samples + k), groups[0][0], dosage)

    two = jnp.stack([factors, cycle(factors, "zh", 1)])
    near = jnp.concatenate([two] + [cycle(two, "x", by) for by in (1, 2, 3)])
    other = cycle(near, "core", 1)
    back = jnp.arange(16)
    from_core = (at["core"] - back // 8) % 2
    from_x = (at["x"] - back // 2 % 4) % 4
    from_zh = (at["zh"] - back % 2) % 2
    order = (from_zh * 8 + from_x * 2 + from_core).astype(jnp.int32)
    fac, inverse, proj, score1, score2 = pl.pallas_call(
        hess_kernel,
        out_shape=(
            jax.ShapeDtypeStruct((k, all_samples), BF16),
            jax.ShapeDtypeStruct((k, k), F32),
            jax.ShapeDtypeStruct((2 * k, snps), BF16),
            table,
            table,
        ),
        in_specs=[pl.BlockSpec(memory_space=pltpu.SMEM), vmem, vmem, vmem, vmem, hbm],
        scratch_shapes=[pltpu.VMEM((k, k), F32), pltpu.VMEM((k, snps), F32)] + tiles,
        cost_estimate=pl.CostEstimate(flops=9_000_000_000, bytes_accessed=10_000_000, transcendentals=0),
        compiler_params=roomy,
        name="hess",
    )(order, near, other, groups[0][1], groups[0][2], dosage)

    back_z = (at["zl"] - jnp.arange(4)) % 4
    back_y = (at["y"] - jnp.arange(4)) % 4
    places = (back_z[None, :] * 4 + back_y[:, None]).astype(jnp.int32).reshape(16)
    slots = (0, 4, 12, 8, 10)
    spots = [(c * width, slot) for c in range(CHUNKS) for slot in slots]
    pieces = [piece for group in groups for piece in group]
    rest = (dosage, fac, inverse, proj)
    out = finish(places, spots[:8], pieces[:8], (score0, score1, score2), *rest, None, width, panel)
    return finish(places, spots[8:], pieces[8:], (), *rest, out, width, panel)


def solution(mesh):
    fine = Mesh(mesh.devices.reshape(2, 4, 2, 4, 4), SAMP + COLS)
    placed = (P(SAMP, COLS), P(COLS, None), P(None, COLS))
    return jax.shard_map(body, mesh=fine, in_specs=placed, out_specs=P(None, SAMP, None, COLS), check_vma=False)
```

```python
import functools

import jax
import jax.numpy as jnp
from jax import lax
from jax.experimental import pallas as pl
from jax.experimental.pallas import tpu as pltpu
from jax.sharding import Mesh, PartitionSpec as P

ridge_factor = 1.0
ridge_sample = 1.0
SAMP = ("zh", "x", "core")
COLS = ("zl", "y")
CHUNKS = 2
F32 = jnp.float32
BF16 = jnp.bfloat16
HI = lax.Precision.HIGHEST
NT = (((1,), (1,)), ((), ()))
TN = (((0,), (0,)), ((), ()))


def cycle(array, axis, by):
    size = lax.axis_size(axis)
    return lax.ppermute(array, axis, [(i, (i + by) % size) for i in range(size)])


def invert2(a, b, c):
    r = 1.0 / (a * c - b * b)
    return c * r, -b * r, a * r


def sweep(a_ref, beside):
    n = a_ref.shape[0]
    ci = lax.broadcasted_iota(jnp.int32, (n, n), 1)
    lane = ci[:1]

    def step(t, _):
        k = 4 * t
        beside(t, True)
        a = a_ref[...]
        r = [a_ref[pl.ds(k + i, 1), :] for i in range(4)]
        c = [jnp.sum(jnp.where(ci == k + i, a, 0.0), axis=1, keepdims=True) for i in range(4)]
        b = [[None] * i + [jnp.sum(jnp.where(lane == k + j, r[i], 0.0), axis=1, keepdims=True) for j in range(i, 4)] for i in range(4)]
        s11, s12, s22 = invert2(b[0][0], b[0][1], b[1][1])
        q11, q12, q21, q22 = b[0][2], b[0][3], b[1][2], b[1][3]
        w11, w12 = s11 * q11 + s12 * q21, s11 * q12 + s12 * q22
        w21, w22 = s12 * q11 + s22 * q21, s12 * q12 + s22 * q22
        t11, t12, t22 = invert2(
            b[2][2] - (q11 * w11 + q21 * w21), b[2][3] - (q11 * w12 + q21 * w22), b[3][3] - (q12 * w12 + q22 * w22)
        )
        m11, m12 = -(w11 * t11 + w12 * t12), -(w11 * t12 + w12 * t22)
        m21, m22 = -(w21 * t11 + w22 * t12), -(w21 * t12 + w22 * t22)
        l11, l12 = s11 - (m11 * w11 + m12 * w12), s12 - (m11 * w21 + m12 * w22)
        l22 = s22 - (m21 * w21 + m22 * w22)
        inv = [[l11, l12, m11, m12], [l12, l22, m21, m22], [m11, m21, t11, t12], [m12, m22, t12, t22]]
        p = [(inv[i][0] * r[0] + inv[i][1] * r[1]) + (inv[i][2] * r[2] + inv[i][3] * r[3]) for i in range(4)]
        new = a - ((c[0] * p[0] + c[1] * p[1]) + (c[2] * p[2] + c[3] * p[3]))
        for i in range(4):
            q = (inv[i][0] * c[0] + inv[i][1] * c[1]) + (inv[i][2] * c[2] + inv[i][3] * c[3])
            new = jnp.where(ci == k + i, q, new)
        a_ref[...] = new
        for i in range(4):
            for j in range(4):
                p[i] = jnp.where(lane == k + j, -inv[i][j], p[i])
            a_ref[pl.ds(k + i, 1), :] = p[i]
        beside(t)
        return 0

    lax.fori_loop(0, n // 4, step, 0)


def eye(n):
    ri = lax.broadcasted_iota(jnp.int32, (n, n), 0)
    return jnp.where(ri == lax.broadcasted_iota(jnp.int32, (n, n), 1), 1.0, 0.0).astype(F32)


STEPS = 32
TILE = 256


class Products:
    def __init__(self, dos_hbm, dos, sems):
        self.dos = dos
        self.copies = [
            pltpu.make_async_copy(
                dos_hbm.at[:, pl.ds(n * TILE, TILE)], dos.at[:, pl.ds(n * TILE, TILE)], sems.at[n]
            )
            for n in range(dos.shape[1] // TILE)
        ]
        self.shares = STEPS // len(self.copies)
        self.pairs = []
        for copy in self.copies:
            copy.start()

    def __call__(self, t, before=False):
        if before:
            for n, copy in enumerate(self.copies):
                pl.when(t == n * self.shares)(copy.wait)
            return
        depth = self.dos.shape[0] // self.shares
        part = lax.rem(t, self.shares)
        inner = pl.ds(pl.multiple_of(part * depth, depth), depth)
        column = pl.ds(pl.multiple_of(lax.div(t, self.shares) * TILE, TILE), TILE)
        tile = self.dos[inner, column]
        for rows, out in self.pairs:
            found = jnp.dot(rows[:, inner], tile, preferred_element_type=F32)
            out[:, column] = jnp.where(part == 0, found, out[:, column] + found)


def factor_kernel(sums_ref, rows, dos_hbm, out_ref, score, mat, dos, sems):
    k = sums_ref.shape[0]
    products = Products(dos_hbm, dos, sems)
    products.pairs = [(rows, score)]
    mat[...] = sums_ref[:, -k:] + ridge_factor * eye(k)
    sweep(mat, products)
    found = jnp.dot(-mat[...], sums_ref[:, :-k], preferred_element_type=F32, precision=HI)
    out_ref[...] = found.astype(BF16)


def hess_kernel(places, near, other, ahead, behind, dos_hbm, fac, inverse, proj, score1, score2, mat, total, dos, sems):
    k = mat.shape[0]
    width = near.shape[2]
    products = Products(dos_hbm, dos, sems)
    products.pairs = [(fac, total), (ahead, score1), (behind, score2)]
    for i in range(8):
        fac[:, pl.ds(pl.multiple_of(places[i] * width, width), width)] = near[i]
        fac[:, pl.ds(pl.multiple_of(places[8 + i] * width, width), width)] = other[i]
    mat[...] = lax.dot_general(fac[...], fac[...], NT, preferred_element_type=F32) + ridge_sample * eye(k)
    sweep(mat, products)
    inverse[...] = -mat[...]
    found = total[...]
    high = found.astype(BF16)
    proj[:k, :] = high
    proj[k:, :] = (found - high.astype(F32)).astype(BF16)


def finish_kernel(scale, genes, spots, sizes, given, places, *refs):
    count = len(spots)
    pieces, scores = refs[:count], refs[count : count + given]
    dos, fac, inverse, proj = refs[count + given : count + given + 4]
    out, held, done, coef, loads, sems = refs[-6:]
    n = pl.program_id(0)
    spans = [(sum(sizes[:i]), size) for i, size in enumerate(sizes)]
    known = sum(sizes[:given])

    @pl.when(n == 0)
    def _():
        copies = [
            pltpu.make_async_copy(piece, held.at[pl.ds(at, size), :], loads.at[i])
            for i, (piece, (at, size)) in enumerate(zip(pieces, spans))
        ]
        for copy in copies:
            copy.start()
        for copy, (at, size) in zip(copies, spans):
            copy.wait()
            cross = lax.dot_general(held[pl.ds(at, size), :], fac[...], NT, preferred_element_type=F32)
            half = jnp.dot(cross, inverse[...], preferred_element_type=F32, precision=HI).astype(BF16)
            coef[pl.ds(at, size), :] = jnp.concatenate([half, half], axis=1)

    column = pl.ds(pl.multiple_of(n * TILE, TILE), TILE)
    for score, (at, size) in zip(scores, spans):
        rows = pl.ds(at, size)
        total = score[...] - jnp.dot(coef[rows, :], proj[...], preferred_element_type=F32)
        done[rows, column] = (total * scale).astype(BF16)
    total = jnp.dot(held[known:, :], dos[...], preferred_element_type=F32)
    total -= jnp.dot(coef[known:, :], proj[...], preferred_element_type=F32)
    done[known:, column] = (total * scale).astype(BF16)

    @pl.when(n == pl.num_programs(0) - 1)
    def _():
        copies = []
        for (start, slot), (at, size) in zip(spots, spans):
            for i in range(size // genes):
                copies.append(
                    pltpu.make_async_copy(
                        done.at[pl.ds(at + i * genes, genes), :],
                        out.at[places[slot + i], 0, pl.ds(start, genes), :],
                        sems.at[at // genes + i],
                    )
                )
        for copy in copies:
            copy.start()
        for copy in copies:
            copy.wait()


def finish(places, spots, pieces, scores, dosage, fac, inverse, proj, out, genes, panel):
    samples, snps = dosage.shape
    sizes = tuple(p.shape[0] for p in pieces)
    rows = sum(sizes)
    fixed = lambda a: pl.BlockSpec(a.shape, lambda n, _: (0, 0), pipeline_mode=pl.Buffered(1))
    across = lambda a: pl.BlockSpec((a.shape[0], TILE), lambda n, _: (0, n))
    left = pl.BlockSpec(memory_space=pl.ANY)
    ins = list(pieces) + list(scores) + [dosage, fac, inverse, proj]
    specs = [left for _ in pieces] + [across(a) for a in scores]
    specs += [across(dosage), fixed(fac), fixed(inverse), across(proj)]
    alias = {}
    if out is not None:
        alias = {len(ins) + 1: 0}
        ins.append(out)
        specs.append(left)
    return pl.pallas_call(
        functools.partial(finish_kernel, float(samples) ** -0.5, genes, spots, sizes, len(scores)),
        out_shape=jax.ShapeDtypeStruct((16, 1, panel, snps), BF16),
        grid_spec=pltpu.PrefetchScalarGridSpec(
            num_scalar_prefetch=1,
            grid=(snps // TILE,),
            in_specs=specs,
            out_specs=left,
            scratch_shapes=[
                pltpu.VMEM((rows, samples), BF16),
                pltpu.VMEM((rows, snps), BF16),
                pltpu.VMEM((rows, proj.shape[0]), BF16),
                pltpu.SemaphoreType.DMA((len(pieces),)),
                pltpu.SemaphoreType.DMA((rows // genes,)),
            ],
        ),
        input_output_aliases=alias,
        cost_estimate=pl.CostEstimate(flops=2 * rows * samples * 1024, bytes_accessed=rows * 16384, transcendentals=0),
    )(places, *ins)


def body(expression, loadings, dosage):
    samples, genes = expression.shape
    k = loadings.shape[1]
    n_samp, n_cols = lax.axis_size(SAMP), lax.axis_size(COLS)
    panel = genes // n_samp
    all_samples, snps = dosage.shape
    at = {name: lax.axis_index(name) for name in SAMP + COLS}

    flipped = expression.T
    mine = lax.all_to_all(flipped.reshape(n_samp, panel, samples), SAMP, 0, 0, tiled=True)
    mine = mine.transpose(1, 0, 2).reshape(panel, all_samples)

    both = jnp.concatenate(
        [
            lax.dot_general(loadings, flipped, TN, preferred_element_type=F32),
            lax.dot_general(loadings, loadings, TN, preferred_element_type=F32),
        ],
        axis=1,
    )
    both = lax.all_to_all(both.reshape(n_cols, k // n_cols, samples + k), COLS, 0, 0, tiled=True)
    both = both.sum(axis=0)
    both = lax.all_to_all(jnp.broadcast_to(both[None], (n_cols,) + both.shape), COLS, 0, 0, tiled=True)
    width = panel // CHUNKS
    groups = []
    for c in range(CHUNKS):
        piece = mine[c * width : c * width + width]
        along = [piece] + [cycle(piece, "zl", by) for by in (1, 2, 3)]
        own = jnp.concatenate(along)
        ahead, behind = cycle(own, "y", 1), cycle(own, "y", -1)
        low, high = ahead[: 2 * width], behind[2 * width :]
        low, high = cycle(low, "y", 1), cycle(high, "y", -1)
        groups.append((own, ahead, behind, low, high))

    vmem, hbm = pl.BlockSpec(memory_space=pltpu.VMEM), pl.BlockSpec(memory_space=pltpu.HBM)
    table = jax.ShapeDtypeStruct((4 * width, snps), F32)
    tiles = [pltpu.VMEM(dosage.shape, BF16), pltpu.SemaphoreType.DMA((snps // TILE,))]
    factors, score0 = pl.pallas_call(
        factor_kernel,
        out_shape=(jax.ShapeDtypeStruct((k, samples), BF16), table),
        in_specs=[vmem, vmem, hbm],
        scratch_shapes=[pltpu.VMEM((k, k), F32)] + tiles,
        cost_estimate=pl.CostEstimate(flops=7_000_000_000, bytes_accessed=400_000, transcendentals=0),
        name="factor",
    )(both.reshape(k, samples + k), groups[0][0], dosage)

    two = jnp.stack([factors, cycle(factors, "zh", 1)])
    near = jnp.concatenate([two] + [cycle(two, "x", by) for by in (1, 2, 3)])
    other = cycle(near, "core", 1)
    back = jnp.arange(16)
    from_core = (at["core"] - back // 8) % 2
    from_x = (at["x"] - back // 2 % 4) % 4
    from_zh = (at["zh"] - back % 2) % 2
    order = (from_zh * 8 + from_x * 2 + from_core).astype(jnp.int32)
    fac, inverse, proj, score1, score2 = pl.pallas_call(
        hess_kernel,
        out_shape=(
            jax.ShapeDtypeStruct((k, all_samples), BF16),
            jax.ShapeDtypeStruct((k, k), F32),
            jax.ShapeDtypeStruct((2 * k, snps), BF16),
            table,
            table,
        ),
        in_specs=[pl.BlockSpec(memory_space=pltpu.SMEM), vmem, vmem, vmem, vmem, hbm],
        scratch_shapes=[pltpu.VMEM((k, k), F32), pltpu.VMEM((k, snps), F32)] + tiles,
        cost_estimate=pl.CostEstimate(flops=9_000_000_000, bytes_accessed=10_000_000, transcendentals=0),
        name="hess",
    )(order, near, other, groups[0][1], groups[0][2], dosage)

    back_z = (at["zl"] - jnp.arange(4)) % 4
    back_y = (at["y"] - jnp.arange(4)) % 4
    places = (back_z[None, :] * 4 + back_y[:, None]).astype(jnp.int32).reshape(16)
    slots = (0, 4, 12, 8, 10)
    spots = [(c * width, slot) for c in range(CHUNKS) for slot in slots]
    pieces = [piece for group in groups for piece in group]
    rest = (dosage, fac, inverse, proj)
    out = finish(places, spots[:8], pieces[:8], (score0, score1, score2), *rest, None, width, panel)
    return finish(places, spots[8:], pieces[8:], (), *rest, out, width, panel)


def solution(mesh):
    fine = Mesh(mesh.devices.reshape(2, 4, 2, 4, 4), SAMP + COLS)
    placed = (P(SAMP, COLS), P(COLS, None), P(None, COLS))
    return jax.shard_map(body, mesh=fine, in_specs=placed, out_specs=P(None, SAMP, None, COLS), check_vma=False)
```

```python
import functools

import jax
import jax.numpy as jnp
from jax import lax
from jax.experimental import pallas as pl
from jax.experimental.pallas import tpu as pltpu
from jax.sharding import Mesh, PartitionSpec as P

ridge_factor = 1.0
ridge_sample = 1.0
SAMP = ("zh", "x", "core")
COLS = ("zl", "y")
CHUNKS = 2
F32 = jnp.float32
BF16 = jnp.bfloat16
HI = lax.Precision.HIGHEST
NT = (((1,), (1,)), ((), ()))
TN = (((0,), (0,)), ((), ()))


def cycle(array, axis, by):
    size = lax.axis_size(axis)
    return lax.ppermute(array, axis, [(i, (i + by) % size) for i in range(size)])


def invert2(a, b, c):
    r = 1.0 / (a * c - b * b)
    return c * r, -b * r, a * r


def sweep(a_ref):
    n = a_ref.shape[0]
    ci = lax.broadcasted_iota(jnp.int32, (n, n), 1)
    lane = ci[:1]

    def step(t, _):
        k = 4 * t
        a = a_ref[...]
        r = [a_ref[pl.ds(k + i, 1), :] for i in range(4)]
        c = [jnp.sum(jnp.where(ci == k + i, a, 0.0), axis=1, keepdims=True) for i in range(4)]
        b = [[None] * i + [jnp.sum(jnp.where(lane == k + j, r[i], 0.0), axis=1, keepdims=True) for j in range(i, 4)] for i in range(4)]
        s11, s12, s22 = invert2(b[0][0], b[0][1], b[1][1])
        q11, q12, q21, q22 = b[0][2], b[0][3], b[1][2], b[1][3]
        w11, w12 = s11 * q11 + s12 * q21, s11 * q12 + s12 * q22
        w21, w22 = s12 * q11 + s22 * q21, s12 * q12 + s22 * q22
        t11, t12, t22 = invert2(
            b[2][2] - (q11 * w11 + q21 * w21), b[2][3] - (q11 * w12 + q21 * w22), b[3][3] - (q12 * w12 + q22 * w22)
        )
        m11, m12 = -(w11 * t11 + w12 * t12), -(w11 * t12 + w12 * t22)
        m21, m22 = -(w21 * t11 + w22 * t12), -(w21 * t12 + w22 * t22)
        l11, l12 = s11 - (m11 * w11 + m12 * w12), s12 - (m11 * w21 + m12 * w22)
        l22 = s22 - (m21 * w21 + m22 * w22)
        inv = [[l11, l12, m11, m12], [l12, l22, m21, m22], [m11, m21, t11, t12], [m12, m22, t12, t22]]
        p = [(inv[i][0] * r[0] + inv[i][1] * r[1]) + (inv[i][2] * r[2] + inv[i][3] * r[3]) for i in range(4)]
        new = a - ((c[0] * p[0] + c[1] * p[1]) + (c[2] * p[2] + c[3] * p[3]))
        for i in range(4):
            q = (inv[i][0] * c[0] + inv[i][1] * c[1]) + (inv[i][2] * c[2] + inv[i][3] * c[3])
            new = jnp.where(ci == k + i, q, new)
        a_ref[...] = new
        for i in range(4):
            for j in range(4):
                p[i] = jnp.where(lane == k + j, -inv[i][j], p[i])
            a_ref[pl.ds(k + i, 1), :] = p[i]
        return 0

    lax.fori_loop(0, n // 4, step, 0)


def eye(n):
    ri = lax.broadcasted_iota(jnp.int32, (n, n), 0)
    return jnp.where(ri == lax.broadcasted_iota(jnp.int32, (n, n), 1), 1.0, 0.0).astype(F32)


def factor_kernel(sums_ref, out_ref, mat):
    k = sums_ref.shape[0]
    mat[...] = sums_ref[:, -k:] + ridge_factor * eye(k)
    sweep(mat)
    found = jnp.dot(-mat[...], sums_ref[:, :-k], preferred_element_type=F32, precision=HI)
    out_ref[...] = found.astype(BF16)


def hess_kernel(places, *refs):
    parts, (dos_hbm, fac, inverse, proj, mat, dos, sem) = refs[:-7], refs[-7:]
    k = mat.shape[0]
    each, width = parts[0].shape[0], parts[0].shape[2]
    fetch = pltpu.make_async_copy(dos_hbm, dos, sem)
    fetch.start()
    for i, part in enumerate(parts):
        for j in range(each):
            fac[:, pl.ds(pl.multiple_of(places[each * i + j] * width, width), width)] = part[j]
    mat[...] = lax.dot_general(fac[...], fac[...], NT, preferred_element_type=F32) + ridge_sample * eye(k)
    sweep(mat)
    inverse[...] = -mat[...]
    fetch.wait()
    total = jnp.dot(fac[...], dos[...], preferred_element_type=F32)
    high = total.astype(BF16)
    proj[:k, :] = high
    proj[k:, :] = (total - high.astype(F32)).astype(BF16)


def finish_kernel(scale, start, genes, count, places, *refs):
    pieces, scores = refs[:count], refs[count : 2 * count]
    fac, inverse, proj = refs[2 * count : 2 * count + 3]
    out, done, loads, sems = refs[-2 * count - 4], refs[-2 * count - 3], refs[-2 * count - 2], refs[-2 * count - 1]
    held, base = refs[-2 * count : -count], refs[-count:]
    fetches = [pltpu.make_async_copy(a, b, loads.at[i]) for i, (a, b) in enumerate(zip(pieces, held))]
    fetches += [pltpu.make_async_copy(a, b, loads.at[count + i]) for i, (a, b) in enumerate(zip(scores, base))]
    for i in range(count):
        fetches[i].start()
        fetches[count + i].start()
    at, copies = 0, []
    for i in range(count):
        rows = held[i].shape[0]
        fetches[i].wait()
        cross = lax.dot_general(held[i][...], fac[...], NT, preferred_element_type=F32)
        half = jnp.dot(cross, inverse[...], preferred_element_type=F32, precision=HI).astype(BF16)
        coef = jnp.concatenate([half, half], axis=1)
        fetches[count + i].wait()
        total = base[i][...] - jnp.dot(coef, proj[...], preferred_element_type=F32)
        done[pl.ds(at, rows), :] = (total * scale).astype(BF16)
        for j in range(at // genes, (at + rows) // genes):
            copy = pltpu.make_async_copy(
                done.at[pl.ds(j * genes, genes), :], out.at[places[j], 0, pl.ds(start, genes), :], sems.at[j]
            )
            copy.start()
            copies.append(copy)
        at += rows
    for copy in copies:
        copy.wait()


def finish(places, pieces, scores, fac, inverse, proj, out, start, genes, panel, samples):
    snps = scores[0].shape[1]
    rows = sum(p.shape[0] for p in pieces)
    ins = list(pieces) + list(scores) + [fac, inverse, proj]
    specs = [pl.BlockSpec(memory_space=pl.ANY)] * (2 * len(pieces))
    specs += [pl.BlockSpec(a.shape, lambda n, _, nd=a.ndim: (0,) * nd) for a in ins[-3:]]
    alias = {}
    if out is not None:
        alias = {len(ins) + 1: 0}
        ins.append(out)
        specs.append(pl.BlockSpec(memory_space=pl.ANY))
    return pl.pallas_call(
        functools.partial(finish_kernel, float(samples) ** -0.5, start, genes, len(pieces)),
        out_shape=jax.ShapeDtypeStruct((16, 1, panel, snps), BF16),
        grid_spec=pltpu.PrefetchScalarGridSpec(
            num_scalar_prefetch=1,
            grid=(1,),
            in_specs=specs,
            out_specs=pl.BlockSpec(memory_space=pl.ANY),
            scratch_shapes=[
                pltpu.VMEM((rows, snps), BF16),
                pltpu.SemaphoreType.DMA((2 * len(pieces),)),
                pltpu.SemaphoreType.DMA((rows // genes,)),
            ]
            + [pltpu.VMEM(p.shape, BF16) for p in pieces]
            + [pltpu.VMEM(p.shape, F32) for p in scores],
        ),
        input_output_aliases=alias,
        cost_estimate=pl.CostEstimate(flops=2 * rows * samples * 256, bytes_accessed=rows * 16384, transcendentals=0),
        compiler_params=pltpu.CompilerParams(vmem_limit_bytes=30 << 20),
    )(places, *ins)


def body(expression, loadings, dosage):
    samples, genes = expression.shape
    k = loadings.shape[1]
    n_samp, n_cols = lax.axis_size(SAMP), lax.axis_size(COLS)
    panel = genes // n_samp
    all_samples, snps = dosage.shape
    at = {name: lax.axis_index(name) for name in SAMP + COLS}

    flipped = expression.T
    mine = lax.all_to_all(flipped.reshape(n_samp, panel, samples), SAMP, 0, 0, tiled=True)
    mine = mine.transpose(1, 0, 2).reshape(panel, all_samples)

    both = jnp.concatenate(
        [
            lax.dot_general(loadings, expression, (((0,), (1,)), ((), ())), preferred_element_type=F32),
            lax.dot_general(loadings, loadings, TN, preferred_element_type=F32),
        ],
        axis=1,
    )
    both = lax.all_to_all(both.reshape(n_cols, k // n_cols, samples + k), COLS, 0, 0, tiled=True)
    both = both.sum(axis=0)
    both = lax.all_to_all(jnp.broadcast_to(both[None], (n_cols,) + both.shape), COLS, 0, 0, tiled=True)
    factors = pl.pallas_call(
        factor_kernel,
        out_shape=jax.ShapeDtypeStruct((k, samples), BF16),
        scratch_shapes=[pltpu.VMEM((k, k), F32)],
        cost_estimate=pl.CostEstimate(flops=7_000_000_000, bytes_accessed=400_000, transcendentals=0),
        name="factor",
    )(both.reshape(k, samples + k))

    width = panel // CHUNKS
    groups = []
    for c in range(CHUNKS):
        piece = mine[c * width : c * width + width]
        own = jnp.concatenate([piece] + [cycle(piece, "zl", by) for by in (1, 2, 3)])
        ahead, behind = cycle(own, "y", 1), cycle(own, "y", -1)
        if c < CHUNKS - 1:
            far = cycle(ahead, "y", 1)
            groups.append((c * width, [(0, 4), (4, 8), (12, 16), (8, 12)], [own, ahead, behind, far]))
            continue
        low, high = ahead[: 2 * width], behind[2 * width :]
        low, high = cycle(low, "y", 1), cycle(high, "y", -1)
        groups.append((c * width, [(0, 4), (4, 8), (12, 16)], [own, ahead, behind]))
        groups.append((c * width, [(8, 10), (10, 12)], [low, high]))
    scores = []
    for _, _, pieces in groups:
        scores.append([])
        for rows in pieces:
            scores[-1].append(jnp.dot(rows, dosage, preferred_element_type=F32))

    two = jnp.stack([factors, cycle(factors, "zh", 1)])
    four = jnp.concatenate([two, cycle(two, "core", 1)])
    gathered = [four] + [cycle(four, "x", by) for by in (1, 2, 3)]
    back = jnp.arange(16)
    from_core = (at["core"] - back // 2 % 2) % 2
    from_x = (at["x"] - back // 4) % 4
    from_zh = (at["zh"] - back % 2) % 2
    order = (from_zh * 8 + from_x * 2 + from_core).astype(jnp.int32)
    fac, inverse, proj = pl.pallas_call(
        hess_kernel,
        out_shape=(
            jax.ShapeDtypeStruct((k, all_samples), BF16),
            jax.ShapeDtypeStruct((k, k), F32),
            jax.ShapeDtypeStruct((2 * k, snps), BF16),
        ),
        in_specs=[
            pl.BlockSpec(memory_space=pltpu.SMEM),
            *[pl.BlockSpec(memory_space=pltpu.VMEM)] * 4,
            pl.BlockSpec(memory_space=pl.ANY),
        ],
        scratch_shapes=[
            pltpu.VMEM((k, k), F32),
            pltpu.VMEM(dosage.shape, BF16),
            pltpu.SemaphoreType.DMA,
        ],
        cost_estimate=pl.CostEstimate(flops=9_000_000_000, bytes_accessed=10_000_000, transcendentals=0),
        compiler_params=pltpu.CompilerParams(vmem_limit_bytes=24 << 20),
        name="hess",
    )(order, *gathered, dosage)

    back_z = (at["zl"] - jnp.arange(4)) % 4
    back_y = (at["y"] - jnp.arange(4)) % 4
    places = (back_z[None, :] * 4 + back_y[:, None]).astype(jnp.int32).reshape(16)
    out = None
    for (start, slots, pieces), score in zip(groups, scores):
        where = jnp.concatenate([places[a:b] for a, b in slots])
        out = finish(where, pieces, score, fac, inverse, proj, out, start, width, panel, all_samples)
    return out


def solution(mesh):
    fine = Mesh(mesh.devices.reshape(2, 4, 2, 4, 4), SAMP + COLS)
    placed = (P(SAMP, COLS), P(COLS, None), P(None, COLS))
    return jax.shard_map(body, mesh=fine, in_specs=placed, out_specs=P(None, SAMP, None, COLS), check_vma=False)
```

```python
import functools

import jax
import jax.numpy as jnp
from jax import lax
from jax.experimental import pallas as pl
from jax.experimental.pallas import tpu as pltpu
from jax.sharding import Mesh, PartitionSpec as P

ridge_factor = 1.0
ridge_sample = 1.0
SAMP = ("zh", "x", "core")
COLS = ("zl", "y")
CHUNKS = 2
F32 = jnp.float32
BF16 = jnp.bfloat16
HI = lax.Precision.HIGHEST
NT = (((1,), (1,)), ((), ()))
TN = (((0,), (0,)), ((), ()))


def cycle(array, axis, by):
    size = lax.axis_size(axis)
    return lax.ppermute(array, axis, [(i, (i + by) % size) for i in range(size)])


def invert2(a, b, c):
    r = 1.0 / (a * c - b * b)
    return c * r, -b * r, a * r


def sweep(a_ref):
    n = a_ref.shape[0]
    ci = lax.broadcasted_iota(jnp.int32, (n, n), 1)
    lane = ci[:1]

    def step(t, _):
        k = 4 * t
        a = a_ref[...]
        r = [a_ref[pl.ds(k + i, 1), :] for i in range(4)]
        c = [jnp.sum(jnp.where(ci == k + i, a, 0.0), axis=1, keepdims=True) for i in range(4)]
        b = [[None] * i + [jnp.sum(jnp.where(lane == k + j, r[i], 0.0), axis=1, keepdims=True) for j in range(i, 4)] for i in range(4)]
        s11, s12, s22 = invert2(b[0][0], b[0][1], b[1][1])
        q11, q12, q21, q22 = b[0][2], b[0][3], b[1][2], b[1][3]
        w11, w12 = s11 * q11 + s12 * q21, s11 * q12 + s12 * q22
        w21, w22 = s12 * q11 + s22 * q21, s12 * q12 + s22 * q22
        t11, t12, t22 = invert2(
            b[2][2] - (q11 * w11 + q21 * w21), b[2][3] - (q11 * w12 + q21 * w22), b[3][3] - (q12 * w12 + q22 * w22)
        )
        m11, m12 = -(w11 * t11 + w12 * t12), -(w11 * t12 + w12 * t22)
        m21, m22 = -(w21 * t11 + w22 * t12), -(w21 * t12 + w22 * t22)
        l11, l12 = s11 - (m11 * w11 + m12 * w12), s12 - (m11 * w21 + m12 * w22)
        l22 = s22 - (m21 * w21 + m22 * w22)
        inv = [[l11, l12, m11, m12], [l12, l22, m21, m22], [m11, m21, t11, t12], [m12, m22, t12, t22]]
        p = [(inv[i][0] * r[0] + inv[i][1] * r[1]) + (inv[i][2] * r[2] + inv[i][3] * r[3]) for i in range(4)]
        new = a - ((c[0] * p[0] + c[1] * p[1]) + (c[2] * p[2] + c[3] * p[3]))
        for i in range(4):
            q = (inv[i][0] * c[0] + inv[i][1] * c[1]) + (inv[i][2] * c[2] + inv[i][3] * c[3])
            new = jnp.where(ci == k + i, q, new)
        a_ref[...] = new
        for i in range(4):
            for j in range(4):
                p[i] = jnp.where(lane == k + j, -inv[i][j], p[i])
            a_ref[pl.ds(k + i, 1), :] = p[i]
        return 0

    lax.fori_loop(0, n // 4, step, 0)


def eye(n):
    ri = lax.broadcasted_iota(jnp.int32, (n, n), 0)
    return jnp.where(ri == lax.broadcasted_iota(jnp.int32, (n, n), 1), 1.0, 0.0).astype(F32)


def factor_kernel(sums_ref, out_ref, mat):
    k = sums_ref.shape[0]
    mat[...] = sums_ref[:, -k:] + ridge_factor * eye(k)
    sweep(mat)
    found = jnp.dot(-mat[...], sums_ref[:, :-k], preferred_element_type=F32, precision=HI)
    out_ref[...] = found.astype(BF16)


def hess_kernel(places, *refs):
    parts, (dos, fac, inverse, proj, mat) = refs[:-5], refs[-5:]
    k = mat.shape[0]
    each, width = parts[0].shape[0], parts[0].shape[2]
    for i, part in enumerate(parts):
        for j in range(each):
            fac[:, pl.ds(pl.multiple_of(places[each * i + j] * width, width), width)] = part[j]
    mat[...] = lax.dot_general(fac[...], fac[...], NT, preferred_element_type=F32) + ridge_sample * eye(k)
    sweep(mat)
    inverse[...] = -mat[...]
    total = jnp.dot(fac[...], dos[...], preferred_element_type=F32)
    high = total.astype(BF16)
    proj[:k, :] = high
    proj[k:, :] = (total - high.astype(F32)).astype(BF16)


def finish_kernel(scale, start, genes, count, places, *refs):
    pieces, scores = refs[:count], refs[count : 2 * count]
    fac, inverse, proj = refs[2 * count : 2 * count + 3]
    out, done, sems = refs[-3:]
    cross = [lax.dot_general(piece[...], fac[...], NT, preferred_element_type=F32) for piece in pieces]
    cross = jnp.concatenate(cross)
    half = jnp.dot(cross, inverse[...], preferred_element_type=F32, precision=HI).astype(BF16)
    coef = jnp.concatenate([half, half], axis=1)
    at, copies = 0, []
    for score in scores:
        rows = score.shape[0]
        total = score[...] - jnp.dot(coef[at : at + rows], proj[...], preferred_element_type=F32)
        done[pl.ds(at, rows), :] = (total * scale).astype(BF16)
        for i in range(at // genes, (at + rows) // genes):
            copy = pltpu.make_async_copy(
                done.at[pl.ds(i * genes, genes), :], out.at[places[i], 0, pl.ds(start, genes), :], sems.at[i]
            )
            copy.start()
            copies.append(copy)
        at += rows
    for copy in copies:
        copy.wait()


def finish(places, pieces, scores, fac, inverse, proj, out, start, genes, panel, samples):
    snps = scores[0].shape[1]
    rows = sum(p.shape[0] for p in pieces)
    ins = list(pieces) + list(scores) + [fac, inverse, proj]
    specs = [pl.BlockSpec(a.shape, lambda n, _, nd=a.ndim: (0,) * nd) for a in ins]
    alias = {}
    if out is not None:
        alias = {len(ins) + 1: 0}
        ins.append(out)
        specs.append(pl.BlockSpec(memory_space=pl.ANY))
    return pl.pallas_call(
        functools.partial(finish_kernel, float(samples) ** -0.5, start, genes, len(pieces)),
        out_shape=jax.ShapeDtypeStruct((16, 1, panel, snps), BF16),
        grid_spec=pltpu.PrefetchScalarGridSpec(
            num_scalar_prefetch=1,
            grid=(1,),
            in_specs=specs,
            out_specs=pl.BlockSpec(memory_space=pl.ANY),
            scratch_shapes=[pltpu.VMEM((rows, snps), BF16), pltpu.SemaphoreType.DMA((rows // genes,))],
        ),
        input_output_aliases=alias,
        cost_estimate=pl.CostEstimate(flops=2 * rows * samples * 256, bytes_accessed=rows * 16384, transcendentals=0),
        compiler_params=pltpu.CompilerParams(vmem_limit_bytes=30 << 20),
    )(places, *ins)


def body(expression, loadings, dosage):
    samples, genes = expression.shape
    k = loadings.shape[1]
    n_samp, n_cols = lax.axis_size(SAMP), lax.axis_size(COLS)
    panel = genes // n_samp
    all_samples, snps = dosage.shape
    at = {name: lax.axis_index(name) for name in SAMP + COLS}

    flipped = expression.T
    mine = lax.all_to_all(flipped.reshape(n_samp, panel, samples), SAMP, 0, 0, tiled=True)
    mine = mine.transpose(1, 0, 2).reshape(panel, all_samples)

    both = jnp.concatenate(
        [
            lax.dot_general(loadings, expression, (((0,), (1,)), ((), ())), preferred_element_type=F32),
            lax.dot_general(loadings, loadings, TN, preferred_element_type=F32),
        ],
        axis=1,
    )
    both = lax.all_to_all(both.reshape(n_cols, k // n_cols, samples + k), COLS, 0, 0, tiled=True)
    both = both.sum(axis=0)
    both = lax.all_to_all(jnp.broadcast_to(both[None], (n_cols,) + both.shape), COLS, 0, 0, tiled=True)
    factors = pl.pallas_call(
        factor_kernel,
        out_shape=jax.ShapeDtypeStruct((k, samples), BF16),
        scratch_shapes=[pltpu.VMEM((k, k), F32)],
        cost_estimate=pl.CostEstimate(flops=7_000_000_000, bytes_accessed=400_000, transcendentals=0),
        compiler_params=pltpu.CompilerParams(vmem_limit_bytes=8 << 20),
        name="factor",
    )(both.reshape(k, samples + k))

    width = panel // CHUNKS
    groups = []
    for c in range(CHUNKS):
        piece = mine[c * width : c * width + width]
        own = jnp.concatenate([piece] + [cycle(piece, "zl", by) for by in (1, 2, 3)])
        ahead, behind = cycle(own, "y", 1), cycle(own, "y", -1)
        low, high = ahead[: 2 * width], behind[2 * width :]
        low, high = cycle(low, "y", 1), cycle(high, "y", -1)
        near_slots, far_slots = [(0, 4), (4, 8), (12, 16)], [(8, 10), (10, 12)]
        if c < CHUNKS - 1:
            groups.append((c * width, near_slots + far_slots, [own, ahead, behind, low, high]))
        else:
            groups.append((c * width, near_slots, [own, ahead, behind]))
            groups.append((c * width, far_slots, [low, high]))
    scores = []
    for _, _, pieces in groups:
        scores.append([])
        for rows in pieces:
            scores[-1].append(jnp.dot(rows, dosage, preferred_element_type=F32))

    two = jnp.stack([factors, cycle(factors, "zh", 1)])
    four = jnp.concatenate([two, cycle(two, "core", 1)])
    gathered = [four] + [cycle(four, "x", by) for by in (1, 2, 3)]
    back = jnp.arange(16)
    from_core = (at["core"] - back // 2 % 2) % 2
    from_x = (at["x"] - back // 4) % 4
    from_zh = (at["zh"] - back % 2) % 2
    order = (from_zh * 8 + from_x * 2 + from_core).astype(jnp.int32)
    fac, inverse, proj = pl.pallas_call(
        hess_kernel,
        out_shape=(
            jax.ShapeDtypeStruct((k, all_samples), BF16),
            jax.ShapeDtypeStruct((k, k), F32),
            jax.ShapeDtypeStruct((2 * k, snps), BF16),
        ),
        in_specs=[
            pl.BlockSpec(memory_space=pltpu.SMEM),
            *[pl.BlockSpec(memory_space=pltpu.VMEM)] * 5,
        ],
        scratch_shapes=[
            pltpu.VMEM((k, k), F32),
        ],
        cost_estimate=pl.CostEstimate(flops=9_000_000_000, bytes_accessed=10_000_000, transcendentals=0),
        compiler_params=pltpu.CompilerParams(vmem_limit_bytes=24 << 20),
        name="hess",
    )(order, *gathered, dosage)

    back_z = (at["zl"] - jnp.arange(4)) % 4
    back_y = (at["y"] - jnp.arange(4)) % 4
    places = (back_z[None, :] * 4 + back_y[:, None]).astype(jnp.int32).reshape(16)
    out = None
    for (start, slots, pieces), score in zip(groups, scores):
        where = jnp.concatenate([places[a:b] for a, b in slots])
        out = finish(where, pieces, score, fac, inverse, proj, out, start, width, panel, all_samples)
    return out


def solution(mesh):
    fine = Mesh(mesh.devices.reshape(2, 4, 2, 4, 4), SAMP + COLS)
    placed = (P(SAMP, COLS), P(COLS, None), P(None, COLS))
    return jax.shard_map(body, mesh=fine, in_specs=placed, out_specs=P(None, SAMP, None, COLS), check_vma=False)
```
